32 devices in a mesh: trial: 2 (over x), freq: 4 (over y, core), lst: 4 (over z).
Axes of the slice: x: 2, y: 2, z: 4, core: 2. Of those that a mesh axis runs over, the one named last changes fastest.
Arguments:
- sky_east: bfloat16 [8192], P(('trial', 'freq')), parts along dimension 0, may hold values from -0.59765625 to 0.59765625
- sky_north: bfloat16 [8192], P(('trial', 'freq')), parts along dimension 0, may hold values from -0.59765625 to 0.59765625
- sky_flux: bfloat16 [8192], P(('trial', 'freq')), parts along dimension 0, may hold values from 0.19921875 to 5
- sky_scint: bfloat16 [8192, 1024], P(('trial', 'freq'), 'lst'), parts along dimension 0, may hold values from 0.19921875 to 1.796875
- visible: int32 [256, 32], P(('trial', 'lst')), parts along dimension 0, may hold values 0 or 1
- antenna_coords: float32 [350, 2], replicated, may hold values from -150 to 150, as said below
- baseline_antennas: int32 [256, 2], replicated, may hold values from 0 to 349, as said below
- filter_taps: bfloat16 [8, 257], P('freq'), may hold values from -0.375 to 0.375
Outputs:
- visibility: bfloat16 [16, 2, 256, 1024], P(('trial', 'freq'), None, None, 'lst'), parts along dimension 0
- filtered: bfloat16 [16, 2, 256, 1024], P(('trial', 'freq'), None, None, 'lst'), parts along dimension 0
The draws below stay inside these ranges and needn't reach their ends.
There are 2 independent parts, one for each index of `trial`. The reference program is written for one: setup_inputs(seed, part) draws one part's arguments, and reference() takes and returns one part's arrays. A program takes and returns all parts, laid end to end along the dimension named above; an argument that names none is the same for every part. Nothing has to cross between parts.
Inputs may be any that keep to these rules, and one draw needn't show every extreme that they name: `baseline_antennas`: each row names two different antennas. `antenna_coords`: positions in metres; no two antennas are closer than 11 metres.
All inputs are finite; a program needn't handle non-finite values. No bound on the sum of `visible` on one device may be relied on, other than what follows from the above.
Results may differ from the reference program's by a relative error of at most 0.0061.
Values may be sent and summed in bfloat16 or wider, within the bound.
A program may use at most 64 MiB of HBM per device.

```python
import math
import jax
import jax.numpy as jnp
from jax import lax

ANTENNA_COUNT = 350
BASELINE_COUNT = 256
SRC_BLOCK = 128
TAIL = 256
BLOCK_T = 8
TAPS = 257
SOURCES = 4096
CHANNELS = 8
TIME_SAMPLES = 1024
TIME_BLOCKS = 128
SRC_BLOCKS = 32


def draw_antenna_coords(key, part):
    grid_side = int(math.ceil(math.sqrt(ANTENNA_COUNT)))
    index_all = jnp.arange(ANTENNA_COUNT)
    grid_east = (index_all % grid_side).astype(jnp.float32)
    grid_north = (index_all // grid_side).astype(jnp.float32)
    centre_off = 0.5 * (grid_side - 1)
    jitter = jax.random.uniform(jax.random.fold_in(key, 11), (ANTENNA_COUNT, 2), jnp.float32, -2.0, 2.0)
    placed = jnp.stack([15.0 * (grid_east - centre_off), 15.0 * (grid_north - centre_off)], axis=1)
    return (placed + jitter).astype(jnp.float32)


def draw_baseline_antennas(key, part):
    leading_key = jax.random.fold_in(key, 21)
    trailing_key = jax.random.fold_in(key, 22)
    first_antenna = jax.random.randint(leading_key, (BASELINE_COUNT,), 0, ANTENNA_COUNT)
    lag_offsets = jax.random.randint(trailing_key, (BASELINE_COUNT,), 1, ANTENNA_COUNT)
    second_antenna = (first_antenna + lag_offsets) % ANTENNA_COUNT
    return jnp.stack([first_antenna, second_antenna], axis=1).astype(jnp.int32)


def plant(result, own_key, low, top_value):
    longest = result.shape.index(max(result.shape))
    spots = []
    for shift in (0, 1):
        where = [jax.random.randint(jax.random.fold_in(own_key, axis), (), 0, length) for axis, length in enumerate(result.shape)]
        where[longest] = (where[longest] + shift) % result.shape[longest]
        spots.append(tuple(where))
    return result.at[spots[0]].set(low).at[spots[1]].set(top_value)


def block_levels(rng, shape, cuts, least, largest):
    def one(position, blocks):
        draws = jax.random.uniform(jax.random.fold_in(jax.random.fold_in(rng, 6), position), (blocks,), jnp.float32, least / len(cuts), largest / len(cuts))
        return jnp.repeat(jnp.exp(draws), shape[position] // blocks).reshape((-1,) + (1,) * (len(shape) - position - 1))

    gain = one(*cuts[0])
    for cut in cuts[1:]:
        gain = gain * one(*cut)
    return gain


def scatter_about(stream_key, dims, scale, most, shards=(), held_as=jnp.bfloat16):
    result = jax.random.normal(stream_key, dims, jnp.float32) * scale
    if len(shards) > 0:
        result = block_levels(stream_key, dims, shards, -0.22, 0.18) * result
    return jnp.clip(result, min=-most, max=most).astype(held_as)


def setup_inputs(seed: int = 0, part: int = 0) -> dict:
    keys = jax.random.split(jax.random.key(seed), 9)
    own_keys = jax.random.split(jax.random.fold_in(keys[8], part), 9)
    return {
        "sky_east": jnp.clip(jax.random.uniform(own_keys[0], (SOURCES,), jnp.float32, -0.59765625, 0.59765625) * block_levels(own_keys[0], (SOURCES,), ((0, 4),), -0.4, 0.0), -0.59765625, 0.59765625).astype(jnp.bfloat16),
        "sky_north": jnp.clip(jax.random.uniform(own_keys[1], (SOURCES,), jnp.float32, -0.59765625, 0.59765625) * block_levels(own_keys[1], (SOURCES,), ((0, 4),), -0.4, 0.0), -0.59765625, 0.59765625).astype(jnp.bfloat16),
        "sky_flux": jnp.clip(jnp.exp(math.log(5.0) - 3.2227897 * jax.random.uniform(own_keys[2], (SOURCES,), jnp.float32) ** block_levels(own_keys[2], (SOURCES,), ((0, 4),), -0.2, 0.2)), 0.19921875, 5.0).astype(jnp.bfloat16),
        "sky_scint": jnp.clip(0.19921875 + 1.5976562 * jax.random.uniform(own_keys[3], (SOURCES, TIME_SAMPLES), jnp.float32) ** block_levels(own_keys[3], (SOURCES, TIME_SAMPLES), ((0, 4), (1, 4)), -0.2, 0.2), 0.19921875, 1.796875).astype(jnp.bfloat16),
        "visible": plant((jax.random.randint(own_keys[4], (TIME_BLOCKS, SRC_BLOCKS), 0, 4) < 3).astype(jnp.int32), jax.random.fold_in(own_keys[4], 1), 0, 1),
        "antenna_coords": draw_antenna_coords(jax.random.fold_in(keys[8], 71), part),
        "baseline_antennas": draw_baseline_antennas(jax.random.fold_in(keys[8], 71), part),
        "filter_taps": scatter_about(keys[7], (CHANNELS, TAPS), TAPS ** -0.5, 0.375, ((0, 4),)),
    }


C_LIGHT = 299792458.0
NU_START = 150000000.0
NU_STEP = 97656.25
OMEGA_STEP = 4.37526e-05
BEAM_SIGMA = 0.35
CENTRE_START = -0.045
TWO_PI = 2.0 * math.pi

def reference(sky_east, sky_north, sky_flux, sky_scint, visible, antenna_coords, baseline_antennas, filter_taps):
    sky_east = sky_east.astype(jnp.float32)
    sky_north = sky_north.astype(jnp.float32)
    sky_flux = sky_flux.astype(jnp.float32)
    first_antenna = baseline_antennas[:, 0].astype(jnp.int32)
    second_antenna = baseline_antennas[:, 1].astype(jnp.int32)
    baseline_east = antenna_coords[first_antenna, 0] - antenna_coords[second_antenna, 0]
    baseline_north = antenna_coords[first_antenna, 1] - antenna_coords[second_antenna, 1]
    chan_index = jnp.arange(CHANNELS).astype(jnp.int32).astype(jnp.float32)
    frequency = NU_START + NU_STEP * chan_index
    wavenum = TWO_PI * frequency / C_LIGHT
    beam_width = BEAM_SIGMA * NU_START / frequency
    samples = jnp.arange(TIME_SAMPLES).astype(jnp.int32).astype(jnp.float32)
    centre = CENTRE_START + OMEGA_STEP * samples
    seen_mask = jnp.repeat(jnp.repeat(visible.astype(jnp.float32).T, SRC_BLOCK, axis=0), BLOCK_T, axis=1)
    seen_mask = seen_mask * sky_scint.astype(jnp.float32)
    geometry = baseline_east[:, None] * sky_east[None, :] + baseline_north[:, None] * sky_north[None, :]
    scale_norm = 1.0 / math.sqrt(SOURCES)

    def channel(inputs):
        wave, width = inputs
        phases = wave * geometry
        planes = jnp.concatenate([jnp.cos(phases), -jnp.sin(phases)], axis=0).astype(jnp.bfloat16)
        beam_gain = jnp.exp(-((sky_east[:, None] - centre[None, :]) ** 2 + (sky_north ** 2)[:, None]) / (2.0 * width * width))
        amplitude = ((sky_flux * scale_norm)[:, None] * beam_gain * seen_mask).astype(jnp.bfloat16)
        summed_terms = jnp.dot(planes, amplitude, preferred_element_type=jnp.float32)
        real_component = summed_terms[:BASELINE_COUNT]
        imaginary_component = summed_terms[BASELINE_COUNT:]
        fringe = (wave * baseline_east)[:, None] * (OMEGA_STEP * samples)[None, :]
        vis_real = jnp.cos(fringe) * real_component + jnp.sin(fringe) * imaginary_component
        vis_imag = jnp.cos(fringe) * imaginary_component - jnp.sin(fringe) * real_component
        return jnp.stack([vis_real, vis_imag], axis=0).astype(jnp.bfloat16)
    visibility = lax.map(channel, (wavenum, beam_width))

    def smooth(inputs):
        visibility_channel, taps_chan = inputs
        lag_index = jnp.arange(TIME_SAMPLES).astype(jnp.int32)[None, :] - jnp.arange(TIME_SAMPLES).astype(jnp.int32)[:, None]
        inside = (lag_index >= 0) & (lag_index <= TAIL)
        toeplitz = jnp.where(inside, taps_chan[jnp.clip(lag_index, 0, TAIL)], 0.0).astype(jnp.bfloat16)
        every_row = visibility_channel.reshape(2 * BASELINE_COUNT, TIME_SAMPLES)
        filtered_output = jnp.dot(every_row, toeplitz, preferred_element_type=jnp.float32)
        return filtered_output.astype(jnp.bfloat16).reshape(2, BASELINE_COUNT, TIME_SAMPLES)
    filtered = lax.map(smooth, (visibility, filter_taps))
    return (visibility, filtered)
```

```python
import functools
import math

import jax
import jax.numpy as jnp
import numpy as np
from jax import lax
from jax.experimental import pallas as pl
from jax.experimental.pallas import tpu as pltpu
from jax.sharding import PartitionSpec as P

SRC_BLOCK = 128
TAIL = 256
BLOCK_T = 8

C_LIGHT = 299792458.0
NU_START = 150000000.0
NU_STEP = 97656.25
OMEGA_STEP = 4.37526e-05
BEAM_SIGMA = 0.35
CENTRE_START = -0.045
LOG2E = math.log2(math.e)
ROUNDER = 1.5 * 2.0**23
HIDDEN = -1024.0
ROWS = 16
GROUPS = 4
CHUNKS = 4
TILE = 256
MESH = pl.DeviceIdType.MESH
F32 = jnp.float32
BF16 = jnp.bfloat16


def fit_even(fun, reach, degree):
    nodes = np.cos((np.arange(400) + 0.5) * np.pi / 400)
    z = 0.5 * reach * reach * (nodes + 1.0)
    cheb = np.polynomial.chebyshev.Chebyshev.fit(z, fun(np.sqrt(z)), degree, domain=[0.0, reach * reach])
    return [float(c) for c in cheb.convert(kind=np.polynomial.Polynomial).coef]


def cos_turn(x):
    return np.cos(2.0 * np.pi * x)


def sin_turn(x):
    return np.sin(2.0 * np.pi * x) / x


COS_FULL = fit_even(cos_turn, 0.5, 5)
SIN_FULL = fit_even(sin_turn, 0.5, 5)
STEP_REACH = 0.12
COS_STEP = fit_even(cos_turn, STEP_REACH, 3)
SIN_STEP = fit_even(sin_turn, STEP_REACH, 2)


def horner(coefs, z):
    total = coefs[-1] * z + coefs[-2]
    for c in coefs[-3::-1]:
        total = total * z + c
    return total


def sincos_turns(turns):
    r = turns - ((turns + ROUNDER) - ROUNDER)
    z = r * r
    return horner(COS_FULL, z), horner(SIN_FULL, z) * r


def sincos_step(r):
    z = r * r
    return horner(COS_STEP, z), horner(SIN_STEP, z) * r


def pieces(x):
    high = x.astype(BF16).astype(F32)
    middle = (x - high).astype(BF16).astype(F32)
    low = (x - high - middle).astype(BF16).astype(F32)
    return high, middle, low


def rowdot(a, b):
    return lax.dot_general(a, b, (((0,), (0,)), ((), ())), preferred_element_type=F32)


def kernel(
    dims,
    sky_ref, scint_ref, visible_ref, coords_ref, pairs_ref, taps_ref,
    vis_ref, out_ref,
    sky_all, gains_all, phase_rows, beam_rows, planes, amps, mask_rows, coefs, lines, toep, tap_rows, tail,
    sky_send, sky_recv, near_send, near_recv, far_send, far_recv, fwd_send, fwd_recv, halo_send, halo_recv,
):
    n_freq, n_lst, chans, total_sources = dims
    local_src = scint_ref.shape[0]
    times = scint_ref.shape[1]
    count = pairs_ref.shape[0]
    group = count // GROUPS
    chips = n_freq // 2
    part = local_src // CHUNKS
    me = lax.axis_index("freq")
    lst = lax.axis_index("lst")
    chip, core = me // 2, me % 2
    partner = chip * 2 + (1 - core)

    barrier = pltpu.get_barrier_semaphore()
    for d in range(1, n_freq):
        pl.semaphore_signal(barrier, inc=1, device_id={"freq": (me + d) % n_freq}, device_id_type=MESH)

    for d in (1, n_lst - 1):
        pl.semaphore_signal(barrier, inc=1, device_id={"lst": (lst + d) % n_lst}, device_id_type=MESH)
    pl.semaphore_wait(barrier, n_freq + 1)

    def send(src, dst, ssem, rsem, to):
        return pltpu.make_async_remote_copy(
            src_ref=src, dst_ref=dst, send_sem=ssem, recv_sem=rsem, device_id=to, device_id_type=MESH
        )

    sky_copies = [
        send(sky_ref, sky_all.at[me], sky_send.at[d - 1], sky_recv.at[d - 1], {"freq": (me + d) % n_freq})
        for d in range(1, n_freq)
    ]
    for copy in sky_copies:
        copy.start()
    far_copies = []
    for k in range(CHUNKS):
        rows = pl.ds(k * part, part)
        for d in range(1, chips):
            to = ((chip + d) % chips) * 2 + core
            copy = send(
                scint_ref.at[rows], gains_all.at[me, rows], far_send.at[d - 1, k], far_recv.at[d - 1, k], {"freq": to}
            )
            copy.start()
            far_copies.append(copy)
    near_copy = send(scint_ref, gains_all.at[me], near_send.at[0], near_recv.at[0], {"freq": partner})
    near_copy.start()
    sky_all[me] = sky_ref[...]

    first_chan = (me * chans).astype(F32)
    nus = [NU_START + NU_STEP * (first_chan + c) for c in range(chans)]

    antennas = coords_ref.shape[0]
    ids = lax.broadcasted_iota(jnp.int32, (count, antennas), 1)
    select = (pairs_ref[:, 0:1] == ids).astype(F32) - (pairs_ref[:, 1:2] == ids).astype(F32)
    both = jnp.dot(select, coords_ref[...], precision=lax.Precision.HIGHEST, preferred_element_type=F32)
    east, north = both[:, 0:1], both[:, 1:2]
    lane = lax.broadcasted_iota(jnp.int32, (count, ROWS), 1)
    pair_value = jnp.where(lane < 3, east, jnp.where(lane < 6, north, 0.0))

    def coef_rows(scale):
        high, middle, low = pieces(pair_value * scale)
        picked = jnp.where((lane == 0) | (lane == 3), high, jnp.where((lane == 1) | (lane == 4), middle, low))
        return picked.astype(BF16)

    main = coef_rows(nus[0] * (1.0 / C_LIGHT))
    step = coef_rows(NU_STEP / C_LIGHT)
    for g in range(GROUPS):
        coefs[g, 0:group, :] = main[g * group : (g + 1) * group]
        coefs[g, group : 2 * group, :] = step[g * group : (g + 1) * group]
    lines[...] = jnp.broadcast_to(east, lines.shape)

    t_blocks = visible_ref.shape[0]
    spread = (
        lax.broadcasted_iota(jnp.int32, (t_blocks, times), 1) // BLOCK_T
        == lax.broadcasted_iota(jnp.int32, (t_blocks, times), 0)
    ).astype(BF16)
    hidden = ((1.0 - visible_ref[...].astype(F32)) * HIDDEN).astype(BF16)
    mask_rows[...] = rowdot(hidden, spread)

    tap_rows[...] = jnp.zeros_like(tap_rows)
    tap_rows[0:chans, 0 : TAIL + 1] = taps_ref[...].astype(F32)
    for c in range(chans):
        wide = jnp.broadcast_to(tap_rows[c : c + 1, :], (TAIL + times, TAIL + times))
        skewed = pltpu.roll(wide, 0, 1, stride=1, stride_axis=0)
        toep[c] = skewed[:, TAIL:].astype(BF16)

    samples = (lst * times + lax.broadcasted_iota(jnp.int32, (1, times), 1)).astype(F32)
    centre = CENTRE_START + OMEGA_STEP * samples
    row_id = lax.broadcasted_iota(jnp.int32, (ROWS, times), 0)
    beam_right = []
    for c in range(chans):
        ratio = nus[c] * (1.0 / (BEAM_SIGMA * NU_START))
        half = 0.5 * LOG2E * ratio * ratio
        ch, cm, cl = pieces(centre * (2.0 * half))
        gh, gm, gl = pieces(centre * centre * (-half))
        table = jnp.where((row_id >= 3) & (row_id < 6), 1.0, 0.0)
        for at, row in ((0, ch), (1, cm), (2, cl), (6, gh), (7, gm), (8, gl)):
            table = jnp.where(row_id == at, row, table)
        beam_right.append(table)

    for copy in sky_copies:
        copy.wait()

    src_row = lax.broadcasted_iota(jnp.int32, (ROWS, local_src), 0)

    @pl.loop(0, n_freq)
    def _(j):
        l, m, flux = sky_all[j, 0:1, :], sky_all[j, 1:2, :], sky_all[j, 2:3, :]
        cols = pl.ds(pl.multiple_of(j * local_src, local_src), local_src)
        phase_rows[:, cols] = jnp.where(src_row < 3, l, jnp.where(src_row < 6, m, 0.0)).astype(BF16)
        log_flux = jnp.log(flux * (1.0 / math.sqrt(total_sources))) * LOG2E
        for c in range(chans):
            ratio = nus[c] * (1.0 / (BEAM_SIGMA * NU_START))
            half = 0.5 * LOG2E * ratio * ratio
            bh, bm, bl = pieces(log_flux - (l * l + m * m) * half)
            table = jnp.where(src_row < 3, l, 1.0)
            for at, row in ((3, bh), (4, bm), (5, bl)):
                table = jnp.where(src_row == at, row, table)
            beam_rows[c, :, cols] = jnp.where(src_row < 10, table, 0.0).astype(BF16)

    def trig(g):
        @pl.loop(0, total_sources // TILE)
        def _(i):
            cols = pl.ds(pl.multiple_of(i * TILE, TILE), TILE)
            turns = jnp.dot(coefs[g], phase_rows[:, cols], preferred_element_type=F32)
            co, si = sincos_turns(turns[:group])
            cd, sd = sincos_step(turns[group:])
            for c in range(chans):
                if c > 0:
                    co, si = co * cd - si * sd, si * cd + co * sd
                planes[g % 2, c, 0:group, cols] = co.astype(BF16)
                planes[g % 2, c, group : 2 * group, cols] = (-si).astype(BF16)

    def amplitudes(block, gains):
        @pl.loop(0, local_src // SRC_BLOCK)
        def _(k):
            at = pl.multiple_of(block * local_src + k * SRC_BLOCK, SRC_BLOCK)
            mask = mask_rows[pl.ds(block * (local_src // SRC_BLOCK) + k, 1), :]
            gain = gains(pl.ds(pl.multiple_of(k * SRC_BLOCK, SRC_BLOCK), SRC_BLOCK)).astype(F32)
            for c in range(chans):
                right = jnp.where(row_id == 9, mask, beam_right[c]).astype(BF16)
                power = rowdot(beam_rows[c, :, pl.ds(at, SRC_BLOCK)], right)
                amps[c, pl.ds(at, SRC_BLOCK), :] = (jnp.exp2(power) * gain).astype(BF16)

    def multiply(g):
        rows = pl.ds(pl.multiple_of(g * group, group), group)
        for c in range(chans):
            summed = jnp.dot(planes[g % 2, c], amps[c], preferred_element_type=F32)
            real, imag = summed[:group], summed[group:]
            scale = nus[c] * (OMEGA_STEP / C_LIGHT)
            co, si = sincos_turns((lines[rows, :] * scale) * samples)
            vis_ref[c, 0, rows, :] = (co * real + si * imag).astype(BF16)
            vis_ref[c, 1, rows, :] = (co * imag - si * real).astype(BF16)

    def halo(g):
        rows = pl.ds(pl.multiple_of(g * group, group), group)
        return send(
            vis_ref.at[:, :, rows, :], tail.at[:, :, rows, :], halo_send.at[g], halo_recv.at[g], {"lst": (lst + 1) % n_lst}
        )

    def send_group(g):
        @pl.when(lst < n_lst - 1)
        def _():
            halo(g).start()

    def far(d, k):
        rows = pl.ds(k * part, part)
        src = ((chip + chips - d) % chips) * 2 + core
        return send(
            gains_all.at[src, rows], gains_all.at[src, rows], fwd_send.at[d - 1, k], fwd_recv.at[d - 1, k], {"freq": partner}
        )

    def forward(k):
        for d in range(1, chips):
            far_copies[k * (chips - 1) + d - 1].wait_recv()
            far(d, k).start()

    trig(0)
    forward(0)
    amplitudes(me, lambda rows: scint_ref[rows, :])
    near_copy.wait()
    forward(1)
    amplitudes(partner, lambda rows: gains_all[partner, rows, :])
    trig(1)
    for k in range(2, CHUNKS):
        forward(k)
    for d in range(1, chips):
        src = ((chip + chips - d) % chips) * 2 + core
        amplitudes(src, lambda rows, src=src: gains_all[src, rows, :])
    for k in range(CHUNKS):
        for d in range(1, chips):
            far(d, k).wait()
    for d in range(1, chips):
        src = ((chip + chips - d) % chips) * 2 + (1 - core)
        amplitudes(src, lambda rows, src=src: gains_all[src, rows, :])
    for copy in far_copies:
        copy.wait_send()

    @pl.loop(0, GROUPS)
    def _(g):
        multiply(g)
        send_group(g)

        @pl.when(g + 2 < GROUPS)
        def _():
            trig(g + 2)

    @pl.when(lst == 0)
    def _():
        tail[...] = jnp.zeros_like(tail)

    for g in range(GROUPS):
        @pl.when(lst > 0)
        def _():
            halo(g).wait_recv()

        rows = slice(g * group, (g + 1) * group)
        for c in range(chans):
            for r in range(2):
                total = jnp.dot(tail[c, r, rows, :], toep[c, :TAIL, :], preferred_element_type=F32)
                total = total + jnp.dot(vis_ref[c, r, rows, :], toep[c, TAIL:, :], preferred_element_type=F32)
                out_ref[c, r, rows, :] = total.astype(BF16)

    @pl.when(lst < n_lst - 1)
    def _():
        for g in range(GROUPS):
            halo(g).wait_send()


def shards(n_freq, n_lst, sky_east, sky_north, sky_flux, sky_scint, visible, antenna_coords, baseline_antennas, filter_taps):
    chans = filter_taps.shape[0]
    local_src, times = sky_scint.shape
    total = local_src * n_freq
    count = baseline_antennas.shape[0]
    group = count // GROUPS
    chips = n_freq // 2
    sky = jnp.stack([sky_east, sky_north, sky_flux, sky_flux]).astype(F32)
    shape = jax.ShapeDtypeStruct((chans, 2, count, times), BF16)
    vmem = pl.BlockSpec(memory_space=pltpu.VMEM)
    dma = pltpu.SemaphoreType.DMA
    far = max(chips - 1, 1)
    return pl.pallas_call(
        functools.partial(kernel, (n_freq, n_lst, chans, total)),
        out_shape=(shape, shape),
        in_specs=[vmem] * 6,
        out_specs=(vmem, vmem),
        scratch_shapes=[
            pltpu.VMEM((n_freq, 4, local_src), F32),
            pltpu.VMEM((n_freq, local_src, times), BF16),
            pltpu.VMEM((ROWS, total), BF16),
            pltpu.VMEM((chans, ROWS, total), BF16),
            pltpu.VMEM((2, chans, 2 * group, total), BF16),
            pltpu.VMEM((chans, total, times), BF16),
            pltpu.VMEM((visible.shape[1], times), F32),
            pltpu.VMEM((GROUPS, 2 * group, ROWS), BF16),
            pltpu.VMEM((count, times), F32),
            pltpu.VMEM((chans, TAIL + times, times), BF16),
            pltpu.VMEM((8, TAIL + times), F32),
            pltpu.VMEM((chans, 2, count, TAIL), BF16),
            dma((n_freq - 1,)), dma((n_freq - 1,)),
            dma((1,)), dma((1,)),
            dma((far, CHUNKS)), dma((far, CHUNKS)),
            dma((far, CHUNKS)), dma((far, CHUNKS)),
            dma((GROUPS,)), dma((GROUPS,)),
        ],
        compiler_params=pltpu.CompilerParams(
            collective_id=0, has_side_effects=True, vmem_limit_bytes=64000000
        ),
    )(sky, sky_scint, visible, antenna_coords, baseline_antennas, filter_taps)


def solution(mesh):
    return jax.shard_map(
        functools.partial(shards, mesh.shape["freq"], mesh.shape["lst"]),
        mesh=mesh,
        in_specs=(
            P(("trial", "freq")),
            P(("trial", "freq")),
            P(("trial", "freq")),
            P(("trial", "freq"), "lst"),
            P(("trial", "lst"), None),
            P(),
            P(),
            P("freq", None),
        ),
        out_specs=(
            P(("trial", "freq"), None, None, "lst"),
            P(("trial", "freq"), None, None, "lst"),
        ),
        check_vma=False,
    )
```

```python
import functools
import math

import jax
import jax.numpy as jnp
import numpy as np
from jax import lax
from jax.experimental import pallas as pl
from jax.experimental.pallas import tpu as pltpu
from jax.sharding import PartitionSpec as P

SRC_BLOCK = 128
TAIL = 256
BLOCK_T = 8

C_LIGHT = 299792458.0
NU_START = 150000000.0
NU_STEP = 97656.25
OMEGA_STEP = 4.37526e-05
BEAM_SIGMA = 0.35
CENTRE_START = -0.045
LOG2E = math.log2(math.e)
ROUNDER = 1.5 * 2.0**23
HIDDEN = -1024.0
ROWS = 16
GROUPS = 4
CHUNKS = 4
SLOTS = 3
TILE = 256
MESH = pl.DeviceIdType.MESH
F32 = jnp.float32
BF16 = jnp.bfloat16


def fit_even(fun, reach, degree):
    nodes = np.cos((np.arange(400) + 0.5) * np.pi / 400)
    z = 0.5 * reach * reach * (nodes + 1.0)
    cheb = np.polynomial.chebyshev.Chebyshev.fit(z, fun(np.sqrt(z)), degree, domain=[0.0, reach * reach])
    return [float(c) for c in cheb.convert(kind=np.polynomial.Polynomial).coef]


def cos_turn(x):
    return np.cos(2.0 * np.pi * x)


def sin_turn(x):
    return np.sin(2.0 * np.pi * x) / x


COS_FULL = fit_even(cos_turn, 0.5, 5)
SIN_FULL = fit_even(sin_turn, 0.5, 4)
STEP_REACH = 0.12
COS_STEP = fit_even(cos_turn, STEP_REACH, 2)
SIN_STEP = fit_even(sin_turn, STEP_REACH, 2)


def horner(coefs, z):
    total = coefs[-1] * z + coefs[-2]
    for c in coefs[-3::-1]:
        total = total * z + c
    return total


def cos_minus_sin(turns):
    r = turns - ((turns + ROUNDER) - ROUNDER)
    z = r * r
    return horner(COS_FULL, z), horner([-c for c in SIN_FULL], z) * r


def sincos_turns(turns):
    r = turns - ((turns + ROUNDER) - ROUNDER)
    z = r * r
    return horner(COS_FULL, z), horner(SIN_FULL, z) * r


def sincos_step(r):
    z = r * r
    return horner(COS_STEP, z), horner(SIN_STEP, z) * r


def pieces(x):
    high = x.astype(BF16).astype(F32)
    middle = (x - high).astype(BF16).astype(F32)
    low = (x - high - middle).astype(BF16).astype(F32)
    return high, middle, low


def rowdot(a, b):
    return lax.dot_general(a, b, (((0,), (0,)), ((), ())), preferred_element_type=F32)


def kernel(
    dims,
    sky_ref, scint_ref, visible_ref, coords_ref, pairs_ref, taps_ref,
    vis_ref, out_ref,
    sky_all, gains_all, phase_rows, beam_rows, planes, amps, mask_rows, coefs, lines, toep, tap_rows, tail,
    sky_send, sky_recv, near_send, near_recv, far_send, far_recv, fwd_send, fwd_recv, halo_send, halo_recv,
):
    n_freq, n_lst, chans, total_sources = dims
    local_src = scint_ref.shape[0]
    times = scint_ref.shape[1]
    count = pairs_ref.shape[1]
    group = count // GROUPS
    chips = n_freq // 2
    blocks = local_src // SRC_BLOCK
    tiles = total_sources // TILE
    part = local_src // CHUNKS
    me = lax.axis_index("freq")
    lst = lax.axis_index("lst")
    chip, core = me // 2, me % 2
    partner = chip * 2 + (1 - core)

    barrier = pltpu.get_barrier_semaphore()
    for d in range(1, n_freq):
        pl.semaphore_signal(barrier, inc=1, device_id={"freq": (me + d) % n_freq}, device_id_type=MESH)

    for d in (1, n_lst - 1):
        pl.semaphore_signal(barrier, inc=1, device_id={"lst": (lst + d) % n_lst}, device_id_type=MESH)
    pl.semaphore_wait(barrier, n_freq + 1)

    def send(src, dst, ssem, rsem, to):
        return pltpu.make_async_remote_copy(
            src_ref=src, dst_ref=dst, send_sem=ssem, recv_sem=rsem, device_id=to, device_id_type=MESH
        )

    sky_copies = [
        send(sky_ref, sky_all.at[me], sky_send.at[d - 1], sky_recv.at[d - 1], {"freq": (me + d) % n_freq})
        for d in range(1, n_freq)
    ]
    for copy in sky_copies:
        copy.start()
    far_copies = []
    for k in range(CHUNKS):
        rows = pl.ds(k * part, part)
        for d in range(1, chips):
            to = ((chip + d) % chips) * 2 + core
            copy = send(
                scint_ref.at[rows], gains_all.at[me, rows], far_send.at[d - 1, k], far_recv.at[d - 1, k], {"freq": to}
            )
            copy.start()
            far_copies.append(copy)
    near_copy = send(scint_ref, gains_all.at[me], near_send.at[0], near_recv.at[0], {"freq": partner})
    near_copy.start()
    sky_all[me] = sky_ref[...]

    first_chan = (me * chans).astype(F32)
    nus = [NU_START + NU_STEP * (first_chan + c) for c in range(chans)]

    antennas = coords_ref.shape[1]
    ids = lax.broadcasted_iota(jnp.int32, (antennas, count), 0)
    select = (pairs_ref[0:1, :] == ids).astype(F32) - (pairs_ref[1:2, :] == ids).astype(F32)
    both = jnp.dot(coords_ref[...], select, precision=lax.Precision.HIGHEST, preferred_element_type=F32)
    east = jnp.broadcast_to(both[0:1, :], (128, count)).T
    north = jnp.broadcast_to(both[1:2, :], (128, count)).T
    lane = lax.broadcasted_iota(jnp.int32, (count, 128), 1)
    pair_value = jnp.where(lane < 3, east, jnp.where(lane < 6, north, 0.0))

    def coef_rows(scale):
        high, middle, low = pieces(pair_value * scale)
        picked = jnp.where((lane == 0) | (lane == 3), high, jnp.where((lane == 1) | (lane == 4), middle, low))
        return picked.astype(BF16)[:, :ROWS]

    main = coef_rows(nus[0] * (1.0 / C_LIGHT))
    step = coef_rows(NU_STEP / C_LIGHT)
    for g in range(GROUPS):
        coefs[g, 0:group, :] = main[g * group : (g + 1) * group]
        coefs[g, group : 2 * group, :] = step[g * group : (g + 1) * group]
    lines[...] = east

    t_blocks = visible_ref.shape[0]
    spread = (
        lax.broadcasted_iota(jnp.int32, (t_blocks, times), 1) // BLOCK_T
        == lax.broadcasted_iota(jnp.int32, (t_blocks, times), 0)
    ).astype(BF16)
    hidden = ((1.0 - visible_ref[...].astype(F32)) * HIDDEN).astype(BF16)
    mask_rows[...] = rowdot(hidden, spread)

    tap_rows[...] = jnp.zeros_like(tap_rows)
    tap_rows[0:chans, 0 : TAIL + 1] = taps_ref[...].astype(F32)
    for c in range(chans):
        wide = jnp.broadcast_to(tap_rows[c : c + 1, :], (TAIL + times, TAIL + times))
        skewed = pltpu.roll(wide, 0, 1, stride=1, stride_axis=0)
        toep[c] = skewed[:, TAIL:].astype(BF16)

    samples = (lst * times + lax.broadcasted_iota(jnp.int32, (1, times), 1)).astype(F32)
    centre = CENTRE_START + OMEGA_STEP * samples
    row_id = lax.broadcasted_iota(jnp.int32, (ROWS, times), 0)
    beam_right = []
    for c in range(chans):
        ratio = nus[c] * (1.0 / (BEAM_SIGMA * NU_START))
        half = 0.5 * LOG2E * ratio * ratio
        ch, cm, cl = pieces(centre * (2.0 * half))
        gh, gm, gl = pieces(centre * centre * (-half))
        table = jnp.where((row_id >= 3) & (row_id < 6), 1.0, 0.0)
        for at, row in ((0, ch), (1, cm), (2, cl), (6, gh), (7, gm), (8, gl)):
            table = jnp.where(row_id == at, row, table)
        beam_right.append(table)

    for copy in sky_copies:
        copy.wait()

    src_row = lax.broadcasted_iota(jnp.int32, (ROWS, local_src), 0)

    @pl.loop(0, n_freq)
    def _(j):
        l, m, flux = sky_all[j, 0:1, :], sky_all[j, 1:2, :], sky_all[j, 2:3, :]
        cols = pl.ds(pl.multiple_of(j * local_src, local_src), local_src)
        phase_rows[:, cols] = jnp.where(src_row < 3, l, jnp.where(src_row < 6, m, 0.0)).astype(BF16)
        log_flux = jnp.log(flux * (1.0 / math.sqrt(total_sources))) * LOG2E
        for c in range(chans):
            ratio = nus[c] * (1.0 / (BEAM_SIGMA * NU_START))
            half = 0.5 * LOG2E * ratio * ratio
            bh, bm, bl = pieces(log_flux - (l * l + m * m) * half)
            table = jnp.where(src_row < 3, l, 1.0)
            for at, row in ((3, bh), (4, bm), (5, bl)):
                table = jnp.where(src_row == at, row, table)
            beam_rows[c, :, cols] = jnp.where(src_row < 10, table, 0.0).astype(BF16)

    def trig_tile(g, i):
        cols = pl.ds(pl.multiple_of(i * TILE, TILE), TILE)
        turns = jnp.dot(coefs[g], phase_rows[:, cols], preferred_element_type=F32)
        co, si = cos_minus_sin(turns[:group])
        cd, sd = sincos_step(turns[group:])
        for c in range(chans):
            if c > 0:
                co, si = co * cd + si * sd, si * cd - co * sd
            planes[g % SLOTS, c, 0:group, cols] = co.astype(BF16)
            planes[g % SLOTS, c, group : 2 * group, cols] = si.astype(BF16)

    def trig(g, first, last):
        @pl.loop(first, last)
        def _(i):
            trig_tile(g, i)

    def amp_step(block, gains, k):
        at = pl.multiple_of(block * local_src + k * SRC_BLOCK, SRC_BLOCK)
        mask = mask_rows[pl.ds(block * blocks + k, 1), :]
        gain = gains(pl.ds(pl.multiple_of(k * SRC_BLOCK, SRC_BLOCK), SRC_BLOCK)).astype(F32)
        for c in range(chans):
            right = jnp.where(row_id == 9, mask, beam_right[c]).astype(BF16)
            power = rowdot(beam_rows[c, :, pl.ds(at, SRC_BLOCK)], right)
            amps[c, pl.ds(at, SRC_BLOCK), :] = (jnp.exp2(power) * gain).astype(BF16)

    def fused(g, first, per, block, gains):
        @pl.loop(0, blocks)
        def _(k):
            amp_step(block, gains, k)
            for q in range(per):
                trig_tile(g, first + k * per + q)

    def amplitudes(block, gains):
        @pl.loop(0, blocks // 2)
        def _(k):
            amp_step(block, gains, 2 * k)
            amp_step(block, gains, 2 * k + 1)

    def multiply(g):
        rows = pl.ds(pl.multiple_of(g * group, group), group)
        for c in range(chans):
            summed = jnp.dot(planes[g % SLOTS, c], amps[c], preferred_element_type=F32)
            real, imag = summed[:group], summed[group:]
            scale = nus[c] * (OMEGA_STEP / C_LIGHT)
            co, si = sincos_turns((lines[rows, 0:1] * scale) * samples)
            vis_ref[c, 0, rows, :] = (co * real + si * imag).astype(BF16)
            vis_ref[c, 1, rows, :] = (co * imag - si * real).astype(BF16)

    def halo(g):
        rows = pl.ds(pl.multiple_of(g * group, group), group)
        return send(
            vis_ref.at[:, :, rows, :], tail.at[:, :, rows, :], halo_send.at[g], halo_recv.at[g], {"lst": (lst + 1) % n_lst}
        )

    def send_group(g):
        @pl.when(lst < n_lst - 1)
        def _():
            halo(g).start()

    def far(d, k):
        rows = pl.ds(k * part, part)
        src = ((chip + chips - d) % chips) * 2 + core
        return send(
            gains_all.at[src, rows], gains_all.at[src, rows], fwd_send.at[d - 1, k], fwd_recv.at[d - 1, k], {"freq": partner}
        )

    def forward(k):
        for d in range(1, chips):
            far_copies[k * (chips - 1) + d - 1].wait_recv()
            far(d, k).start()

    per = min(2, tiles // blocks)
    fused(0, 0, per, me, lambda rows: scint_ref[rows, :])
    trig(0, per * blocks, tiles)
    near_copy.wait()
    forward(0)
    forward(1)
    fused(1, 0, per, partner, lambda rows: gains_all[partner, rows, :])
    trig(1, per * blocks, tiles)
    forward(2)
    trig(2, 0, tiles - blocks)
    forward(3)
    for d in range(1, chips):
        src = ((chip + chips - d) % chips) * 2 + core
        gains = lambda rows, src=src: gains_all[src, rows, :]
        if d == 1:
            fused(2, tiles - blocks, 1, src, gains)
        else:
            amplitudes(src, gains)
    for k in range(CHUNKS):
        for d in range(1, chips):
            far(d, k).wait()
    for d in range(1, chips):
        src = ((chip + chips - d) % chips) * 2 + (1 - core)
        amplitudes(src, lambda rows, src=src: gains_all[src, rows, :])
    for copy in far_copies:
        copy.wait_send()

    @pl.loop(0, GROUPS)
    def _(g):
        multiply(g)
        send_group(g)

        @pl.when(g == GROUPS - 2)
        def _():
            trig(GROUPS - 1, 0, tiles)

    @pl.when(lst == 0)
    def _():
        tail[...] = jnp.zeros_like(tail)

    for g in range(GROUPS):
        @pl.when(lst > 0)
        def _():
            halo(g).wait_recv()

        rows = slice(g * group, (g + 1) * group)
        for c in range(chans):
            for r in range(2):
                total = jnp.dot(tail[c, r, rows, :], toep[c, :TAIL, :], preferred_element_type=F32)
                total = total + jnp.dot(vis_ref[c, r, rows, :], toep[c, TAIL:, :], preferred_element_type=F32)
                out_ref[c, r, rows, :] = total.astype(BF16)

    @pl.when(lst < n_lst - 1)
    def _():
        for g in range(GROUPS):
            halo(g).wait_send()


def shards(n_freq, n_lst, sky_east, sky_north, sky_flux, sky_scint, visible, antenna_coords, baseline_antennas, filter_taps):
    chans = filter_taps.shape[0]
    local_src, times = sky_scint.shape
    total = local_src * n_freq
    count = baseline_antennas.shape[0]
    group = count // GROUPS
    chips = n_freq // 2
    sky = jnp.stack([sky_east, sky_north, sky_flux, sky_flux]).astype(F32)
    shape = jax.ShapeDtypeStruct((chans, 2, count, times), BF16)
    vmem = pl.BlockSpec(memory_space=pltpu.VMEM)
    dma = pltpu.SemaphoreType.DMA
    far = max(chips - 1, 1)
    return pl.pallas_call(
        functools.partial(kernel, (n_freq, n_lst, chans, total)),
        out_shape=(shape, shape),
        in_specs=[vmem] * 6,
        out_specs=(vmem, vmem),
        scratch_shapes=[
            pltpu.VMEM((n_freq, 4, local_src), F32),
            pltpu.VMEM((n_freq, local_src, times), BF16),
            pltpu.VMEM((ROWS, total), BF16),
            pltpu.VMEM((chans, ROWS, total), BF16),
            pltpu.VMEM((SLOTS, chans, 2 * group, total), BF16),
            pltpu.VMEM((chans, total, times), BF16),
            pltpu.VMEM((visible.shape[1], times), F32),
            pltpu.VMEM((GROUPS, 2 * group, ROWS), BF16),
            pltpu.VMEM((count, 128), F32),
            pltpu.VMEM((chans, TAIL + times, times), BF16),
            pltpu.VMEM((8, TAIL + times), F32),
            pltpu.VMEM((chans, 2, count, TAIL), BF16),
            dma((n_freq - 1,)), dma((n_freq - 1,)),
            dma((1,)), dma((1,)),
            dma((far, CHUNKS)), dma((far, CHUNKS)),
            dma((far, CHUNKS)), dma((far, CHUNKS)),
            dma((GROUPS,)), dma((GROUPS,)),
        ],
        compiler_params=pltpu.CompilerParams(
            collective_id=0, has_side_effects=True, vmem_limit_bytes=64000000
        ),
    )(sky, sky_scint, visible, antenna_coords.T, baseline_antennas.T, filter_taps)


def solution(mesh):
    return jax.shard_map(
        functools.partial(shards, mesh.shape["freq"], mesh.shape["lst"]),
        mesh=mesh,
        in_specs=(
            P(("trial", "freq")),
            P(("trial", "freq")),
            P(("trial", "freq")),
            P(("trial", "freq"), "lst"),
            P(("trial", "lst"), None),
            P(),
            P(),
            P("freq", None),
        ),
        out_specs=(
            P(("trial", "freq"), None, None, "lst"),
            P(("trial", "freq"), None, None, "lst"),
        ),
        check_vma=False,
    )
```

```python
import functools
import math

import jax
import jax.numpy as jnp
import numpy as np
from jax import lax
from jax.experimental import pallas as pl
from jax.experimental.pallas import tpu as pltpu
from jax.sharding import PartitionSpec as P

SRC_BLOCK = 128
TAIL = 256
BLOCK_T = 8

C_LIGHT = 299792458.0
NU_START = 150000000.0
NU_STEP = 97656.25
OMEGA_STEP = 4.37526e-05
BEAM_SIGMA = 0.35
CENTRE_START = -0.045
LOG2E = math.log2(math.e)
ROUNDER = 1.5 * 2.0**23
HIDDEN = -1024.0
ROWS = 16
GROUPS = 4
CHUNKS = 4
SLOTS = 3
TILE = 256
MESH = pl.DeviceIdType.MESH
F32 = jnp.float32
BF16 = jnp.bfloat16


def fit_even(fun, reach, degree):
    nodes = np.cos((np.arange(400) + 0.5) * np.pi / 400)
    z = 0.5 * reach * reach * (nodes + 1.0)
    cheb = np.polynomial.chebyshev.Chebyshev.fit(z, fun(np.sqrt(z)), degree, domain=[0.0, reach * reach])
    return [float(c) for c in cheb.convert(kind=np.polynomial.Polynomial).coef]


def cos_turn(x):
    return np.cos(2.0 * np.pi * x)


def sin_turn(x):
    return np.sin(2.0 * np.pi * x) / x


COS_FULL = fit_even(cos_turn, 0.5, 5)
SIN_FULL = fit_even(sin_turn, 0.5, 4)
STEP_REACH = 0.12
COS_STEP = fit_even(cos_turn, STEP_REACH, 2)
SIN_STEP = fit_even(sin_turn, STEP_REACH, 2)


def horner(coefs, z):
    total = coefs[-1] * z + coefs[-2]
    for c in coefs[-3::-1]:
        total = total * z + c
    return total


def cos_minus_sin(turns):
    r = turns - ((turns + ROUNDER) - ROUNDER)
    z = r * r
    return horner(COS_FULL, z), horner([-c for c in SIN_FULL], z) * r


def sincos_turns(turns):
    r = turns - ((turns + ROUNDER) - ROUNDER)
    z = r * r
    return horner(COS_FULL, z), horner(SIN_FULL, z) * r


def sincos_step(r):
    z = r * r
    return horner(COS_STEP, z), horner(SIN_STEP, z) * r


def pieces(x):
    high = x.astype(BF16).astype(F32)
    middle = (x - high).astype(BF16).astype(F32)
    low = (x - high - middle).astype(BF16).astype(F32)
    return high, middle, low


def rowdot(a, b):
    return lax.dot_general(a, b, (((0,), (0,)), ((), ())), preferred_element_type=F32)


def kernel(
    dims,
    sky_ref, scint_ref, visible_ref, coords_ref, pairs_ref, taps_ref,
    vis_ref, out_ref,
    sky_all, gains_all, phase_rows, beam_rows, planes, last_planes, amps, mask_rows, coefs, lines, toep, tap_rows, tail,
    sky_send, sky_recv, near_send, near_recv, far_send, far_recv, fwd_send, fwd_recv, halo_send, halo_recv, own_sem,
):
    n_freq, n_lst, chans, total_sources = dims
    local_src = scint_ref.shape[0]
    times = scint_ref.shape[1]
    count = pairs_ref.shape[1]
    group = count // GROUPS
    chips = n_freq // 2
    blocks = local_src // SRC_BLOCK
    tiles = total_sources // TILE
    part = local_src // CHUNKS
    me = lax.axis_index("freq")
    lst = lax.axis_index("lst")
    chip, core = me // 2, me % 2
    partner = chip * 2 + (1 - core)

    barrier = pltpu.get_barrier_semaphore()
    for d in range(1, n_freq):
        pl.semaphore_signal(barrier, inc=1, device_id={"freq": (me + d) % n_freq}, device_id_type=MESH)

    for d in (1, n_lst - 1):
        pl.semaphore_signal(barrier, inc=1, device_id={"lst": (lst + d) % n_lst}, device_id_type=MESH)
    pl.semaphore_wait(barrier, n_freq + 1)

    def send(src, dst, ssem, rsem, to):
        return pltpu.make_async_remote_copy(
            src_ref=src, dst_ref=dst, send_sem=ssem, recv_sem=rsem, device_id=to, device_id_type=MESH
        )

    sky_copies = [
        send(sky_ref, sky_all.at[me], sky_send.at[d - 1], sky_recv.at[d - 1], {"freq": (me + d) % n_freq})
        for d in range(1, n_freq)
    ]
    for copy in sky_copies:
        copy.start()
    far_copies = []
    for k in range(CHUNKS):
        rows = pl.ds(k * part, part)
        for d in range(1, chips):
            to = ((chip + d) % chips) * 2 + core
            copy = send(
                scint_ref.at[rows], gains_all.at[me, rows], far_send.at[d - 1, k], far_recv.at[d - 1, k], {"freq": to}
            )
            copy.start()
            far_copies.append(copy)
    near_copy = send(scint_ref, gains_all.at[me], near_send.at[0], near_recv.at[0], {"freq": partner})
    near_copy.start()
    own_copy = pltpu.make_async_copy(scint_ref, gains_all.at[me], own_sem.at[0])
    own_copy.start()
    sky_all[me] = sky_ref[...]

    first_chan = (me * chans).astype(F32)
    nus = [NU_START + NU_STEP * (first_chan + c) for c in range(chans)]

    antennas = coords_ref.shape[1]
    ids = lax.broadcasted_iota(jnp.int32, (antennas, count), 0)
    select = (pairs_ref[0:1, :] == ids).astype(F32) - (pairs_ref[1:2, :] == ids).astype(F32)
    both = jnp.dot(coords_ref[...], select, precision=lax.Precision.HIGHEST, preferred_element_type=F32)
    east = jnp.broadcast_to(both[0:1, :], (128, count)).T
    north = jnp.broadcast_to(both[1:2, :], (128, count)).T
    lane = lax.broadcasted_iota(jnp.int32, (count, 128), 1)
    pair_value = jnp.where(lane < 3, east, jnp.where(lane < 6, north, 0.0))

    def coef_rows(scale):
        high, middle, low = pieces(pair_value * scale)
        picked = jnp.where((lane == 0) | (lane == 3), high, jnp.where((lane == 1) | (lane == 4), middle, low))
        return picked.astype(BF16)[:, :ROWS]

    main = coef_rows(nus[0] * (1.0 / C_LIGHT))
    step = coef_rows(NU_STEP / C_LIGHT)
    for g in range(GROUPS):
        coefs[g, 0:group, :] = main[g * group : (g + 1) * group]
        coefs[g, group : 2 * group, :] = step[g * group : (g + 1) * group]
    lines[...] = east

    t_blocks = visible_ref.shape[0]
    spread = (
        lax.broadcasted_iota(jnp.int32, (t_blocks, times), 1) // BLOCK_T
        == lax.broadcasted_iota(jnp.int32, (t_blocks, times), 0)
    ).astype(BF16)
    hidden = ((1.0 - visible_ref[...].astype(F32)) * HIDDEN).astype(BF16)
    mask_rows[...] = rowdot(hidden, spread)

    tap_rows[...] = jnp.zeros_like(tap_rows)
    tap_rows[0:chans, 0 : TAIL + 1] = taps_ref[...].astype(F32)
    for c in range(chans):
        wide = jnp.broadcast_to(tap_rows[c : c + 1, :], (TAIL + times, TAIL + times))
        skewed = pltpu.roll(wide, 0, 1, stride=1, stride_axis=0)
        toep[c] = skewed[:, TAIL:].astype(BF16)

    samples = (lst * times + lax.broadcasted_iota(jnp.int32, (1, times), 1)).astype(F32)
    centre = CENTRE_START + OMEGA_STEP * samples
    row_id = lax.broadcasted_iota(jnp.int32, (ROWS, times), 0)
    beam_right = []
    for c in range(chans):
        ratio = nus[c] * (1.0 / (BEAM_SIGMA * NU_START))
        half = 0.5 * LOG2E * ratio * ratio
        ch, cm, cl = pieces(centre * (2.0 * half))
        gh, gm, gl = pieces(centre * centre * (-half))
        table = jnp.where((row_id >= 3) & (row_id < 6), 1.0, 0.0)
        for at, row in ((0, ch), (1, cm), (2, cl), (6, gh), (7, gm), (8, gl)):
            table = jnp.where(row_id == at, row, table)
        beam_right.append(table)

    for copy in sky_copies:
        copy.wait()

    src_row = lax.broadcasted_iota(jnp.int32, (ROWS, local_src), 0)

    @pl.loop(0, n_freq)
    def _(j):
        l, m, flux = sky_all[j, 0:1, :], sky_all[j, 1:2, :], sky_all[j, 2:3, :]
        cols = pl.ds(pl.multiple_of(j * local_src, local_src), local_src)
        phase_rows[:, cols] = jnp.where(src_row < 3, l, jnp.where(src_row < 6, m, 0.0)).astype(BF16)
        log_flux = jnp.log(flux * (1.0 / math.sqrt(total_sources))) * LOG2E
        for c in range(chans):
            ratio = nus[c] * (1.0 / (BEAM_SIGMA * NU_START))
            half = 0.5 * LOG2E * ratio * ratio
            bh, bm, bl = pieces(log_flux - (l * l + m * m) * half)
            table = jnp.where(src_row < 3, l, 1.0)
            for at, row in ((3, bh), (4, bm), (5, bl)):
                table = jnp.where(src_row == at, row, table)
            beam_rows[c, :, cols] = jnp.where(src_row < 10, table, 0.0).astype(BF16)

    def trig_tile(g, i):
        store = last_planes if g == GROUPS - 1 else planes.at[g]
        cols = pl.ds(pl.multiple_of(i * TILE, TILE), TILE)
        turns = jnp.dot(coefs[g], phase_rows[:, cols], preferred_element_type=F32)
        co, si = cos_minus_sin(turns[:group])
        cd, sd = sincos_step(turns[group:])
        for c in range(chans):
            if c > 0:
                co, si = co * cd + si * sd, si * cd - co * sd
            store[c, 0:group, cols] = co.astype(BF16)
            store[c, group : 2 * group, cols] = si.astype(BF16)

    def trig(g, first, last):
        @pl.loop(first, last)
        def _(i):
            trig_tile(g, i)

    def amp_step(block, gains, k):
        at = pl.multiple_of(block * local_src + k * SRC_BLOCK, SRC_BLOCK)
        mask = mask_rows[pl.ds(block * blocks + k, 1), :]
        gain = gains(pl.ds(pl.multiple_of(k * SRC_BLOCK, SRC_BLOCK), SRC_BLOCK)).astype(F32)
        for c in range(chans):
            right = jnp.where(row_id == 9, mask, beam_right[c]).astype(BF16)
            power = rowdot(beam_rows[c, :, pl.ds(at, SRC_BLOCK)], right)
            amps[c, pl.ds(at, SRC_BLOCK), :] = (jnp.exp2(power) * gain).astype(BF16)

    def fused(g, first, per, block, gains):
        @pl.loop(0, blocks)
        def _(k):
            amp_step(block, gains, k)
            for q in range(per):
                trig_tile(g, first + k * per + q)

    def amplitudes(block, gains):
        @pl.loop(0, blocks // 2)
        def _(k):
            amp_step(block, gains, 2 * k)
            amp_step(block, gains, 2 * k + 1)

    def multiply(g, store):
        rows = pl.ds(pl.multiple_of(g * group, group), group)
        for c in range(chans):
            summed = jnp.dot(store[c], amps[c], preferred_element_type=F32)
            real, imag = summed[:group], summed[group:]
            scale = nus[c] * (OMEGA_STEP / C_LIGHT)
            co, si = sincos_turns((lines[rows, 0:1] * scale) * samples)
            vis_ref[c, 0, rows, :] = (co * real + si * imag).astype(BF16)
            vis_ref[c, 1, rows, :] = (co * imag - si * real).astype(BF16)

    def halo(g):
        rows = pl.ds(pl.multiple_of(g * group, group), group)
        return send(
            vis_ref.at[:, :, rows, :], tail.at[:, :, rows, :], halo_send.at[g], halo_recv.at[g], {"lst": (lst + 1) % n_lst}
        )

    def send_group(g):
        @pl.when(lst < n_lst - 1)
        def _():
            halo(g).start()

    def far(d, k):
        rows = pl.ds(k * part, part)
        src = ((chip + chips - d) % chips) * 2 + core
        return send(
            gains_all.at[src, rows], gains_all.at[src, rows], fwd_send.at[d - 1, k], fwd_recv.at[d - 1, k], {"freq": partner}
        )

    def forward(k):
        for d in range(1, chips):
            far_copies[k * (chips - 1) + d - 1].wait_recv()
            far(d, k).start()

    per = min(2, tiles // blocks)
    own_copy.wait()
    fused(0, 0, per, me, lambda rows: gains_all[me, rows, :])
    trig(0, per * blocks, tiles)
    near_copy.wait()
    forward(0)
    forward(1)
    fused(1, 0, per, partner, lambda rows: gains_all[partner, rows, :])
    trig(1, per * blocks, tiles)
    forward(2)
    trig(2, 0, tiles - blocks)
    forward(3)
    for d in range(1, chips):
        src = ((chip + chips - d) % chips) * 2 + core
        gains = lambda rows, src=src: gains_all[src, rows, :]
        amplitudes(src, gains)
    for k in range(CHUNKS):
        for d in range(1, chips):
            far(d, k).wait()
    for d in range(1, chips):
        src = ((chip + chips - d) % chips) * 2 + (1 - core)
        amplitudes(src, lambda rows, src=src: gains_all[src, rows, :])
    for copy in far_copies:
        copy.wait_send()

    trig(2, tiles - blocks, tiles)
    ahead = 5

    @pl.loop(0, GROUPS - 1)
    def _(g):
        multiply(g, planes.at[g])
        for q in range(ahead):
            trig_tile(GROUPS - 1, g * ahead + q)
        send_group(g)

    trig(GROUPS - 1, (GROUPS - 1) * ahead, tiles)
    multiply(GROUPS - 1, last_planes)
    send_group(GROUPS - 1)

    @pl.when(lst == 0)
    def _():
        tail[...] = jnp.zeros_like(tail)

    for g in range(GROUPS):
        @pl.when(lst > 0)
        def _():
            halo(g).wait_recv()

        rows = slice(g * group, (g + 1) * group)
        for c in range(chans):
            for r in range(2):
                total = jnp.dot(tail[c, r, rows, :], toep[c, :TAIL, :], preferred_element_type=F32)
                total = total + jnp.dot(vis_ref[c, r, rows, :], toep[c, TAIL:, :], preferred_element_type=F32)
                out_ref[c, r, rows, :] = total.astype(BF16)

    @pl.when(lst < n_lst - 1)
    def _():
        for g in range(GROUPS):
            halo(g).wait_send()


def shards(n_freq, n_lst, sky_east, sky_north, sky_flux, sky_scint, visible, antenna_coords, baseline_antennas, filter_taps):
    chans = filter_taps.shape[0]
    local_src, times = sky_scint.shape
    total = local_src * n_freq
    count = baseline_antennas.shape[0]
    group = count // GROUPS
    chips = n_freq // 2
    sky = jnp.stack([sky_east, sky_north, sky_flux, sky_flux]).astype(F32)
    shape = jax.ShapeDtypeStruct((chans, 2, count, times), BF16)
    vmem = pl.BlockSpec(memory_space=pltpu.VMEM)
    dma = pltpu.SemaphoreType.DMA
    far = max(chips - 1, 1)
    return pl.pallas_call(
        functools.partial(kernel, (n_freq, n_lst, chans, total)),
        out_shape=(shape, shape),
        in_specs=[vmem, pl.BlockSpec(memory_space=pl.ANY)] + [vmem] * 4,
        out_specs=(vmem, vmem),
        scratch_shapes=[
            pltpu.VMEM((n_freq, 4, local_src), F32),
            pltpu.VMEM((n_freq, local_src, times), BF16),
            pltpu.VMEM((ROWS, total), BF16),
            pltpu.VMEM((chans, ROWS, total), BF16),
            pltpu.VMEM((SLOTS, chans, 2 * group, total), BF16),
            pltpu.VMEM((chans, 2 * group, total), BF16),
            pltpu.VMEM((chans, total, times), BF16),
            pltpu.VMEM((visible.shape[1], times), F32),
            pltpu.VMEM((GROUPS, 2 * group, ROWS), BF16),
            pltpu.VMEM((count, 128), F32),
            pltpu.VMEM((chans, TAIL + times, times), BF16),
            pltpu.VMEM((8, TAIL + times), F32),
            pltpu.VMEM((chans, 2, count, TAIL), BF16),
            dma((n_freq - 1,)), dma((n_freq - 1,)),
            dma((1,)), dma((1,)),
            dma((far, CHUNKS)), dma((far, CHUNKS)),
            dma((far, CHUNKS)), dma((far, CHUNKS)),
            dma((GROUPS,)), dma((GROUPS,)), dma((1,)),
        ],
        compiler_params=pltpu.CompilerParams(
            collective_id=0, has_side_effects=True, vmem_limit_bytes=66000000
        ),
    )(sky, sky_scint, visible, antenna_coords.T, baseline_antennas.T, filter_taps)


def solution(mesh):
    return jax.shard_map(
        functools.partial(shards, mesh.shape["freq"], mesh.shape["lst"]),
        mesh=mesh,
        in_specs=(
            P(("trial", "freq")),
            P(("trial", "freq")),
            P(("trial", "freq")),
            P(("trial", "freq"), "lst"),
            P(("trial", "lst"), None),
            P(),
            P(),
            P("freq", None),
        ),
        out_specs=(
            P(("trial", "freq"), None, None, "lst"),
            P(("trial", "freq"), None, None, "lst"),
        ),
        check_vma=False,
    )
```
